32 devices in a mesh: groups: 1, wide: 32 (over z, y, x, core).
Axes of the slice: x: 2, y: 2, z: 4, core: 2. Of those that a mesh axis runs over, the one named last changes fastest.
Arguments:
- queries: bfloat16 [2, 1024, 4096], P('groups', 'wide'), may hold values from -100 to 100
- key_rows: bfloat16 [2, 1024, 1024], P('groups', 'wide'), may hold values from -5 to 5
- value_rows: bfloat16 [2, 1024, 1024], P('groups', 'wide'), may hold values from -5 to 5
- residual: bfloat16 [2, 1024, 4096], P('groups', 'wide'), may hold values from -4 to 4
- segment_ids: int32 [2048], P('groups'), may hold values from 0 to 47, never falling along the last dimension, each value on 1 to 64 neighbouring positions
- routes: int32 [2, 1024, 2], P('groups', 'wide'), may hold values from 0 to 15, all different within a row; in each aligned block of 32 rows (0 to 31, 32 to 63, ..., all dimensions but the last counted through in order) at most 5 rows name the same one
- route_weights: float32 [2, 1024, 2], P('groups', 'wide'), may hold values from 0.1 to 1
- norm_gain: float32 [4096], replicated, may hold values from 0.5 to 1.5
- norm_bias: float32 [4096], replicated, may hold values from -3 to 3
- w_gate: bfloat16 [4096, 51200], P(None, 'wide'), may hold values from -0.09375 to 0.09375
- w_up: bfloat16 [4096, 51200], P(None, 'wide'), may hold values from -0.09375 to 0.09375
- w_down: bfloat16 [51200, 4096], P('wide'), may hold values from -0.109375 to 0.109375
Outputs:
- layer_out: bfloat16 [2, 1024, 4096], P('groups', 'wide')
The draws below stay inside these ranges and needn't reach their ends.
Inputs may be any that keep to these rules, and one draw needn't show every extreme that they name: `routes`: the 2 experts of a row differ. In each micro-batch, no expert is named more than 5 times by the rows of one device, and in every draw some expert is named exactly 5 times by one device's rows. `segment_ids`: never falls along the positions; no document has more than 64 positions, and one has exactly 64.
All inputs are finite; a program needn't handle non-finite values.
Results may differ from the reference program's by a relative error of at most 0.012.
Values may be sent and summed in bfloat16 or wider, within the bound.
A program may use at most 128 MiB of HBM per device.

```python
import math
import jax
import jax.numpy as jnp
import numpy as np
from jax import lax

D = 4096
HEADS = 32
KVH = 8
HD = 128
EXPERTS = 16
FF = 3200
TOP = 2
MB = 2
DOCS = 48
TOKENS = 2048
TOKM = 1024
TOKM_DEV = 32
C = 5
FF_DEV = 1600
DOC_MOST = 64
N_WIDE = 32


def shared_rows(key):
    base = jax.random.fold_in(key, 11)
    first, second = jax.random.split(base, 2)
    keys_drawn = jax.random.truncated_normal(first, -4.0, 4.0, (MB, TOKM, KVH * HD), jnp.float32)
    queries_drawn = jax.random.truncated_normal(second, -4.0, 4.0, (MB, TOKM, HEADS * HD), jnp.float32)
    return (queries_drawn, keys_drawn)


def draw_queries(key, part):
    queries_drawn, keys_drawn = shared_rows(key)
    return queries_drawn.astype(jnp.bfloat16)


def draw_key_rows(key, part):
    queries_drawn, keys_drawn = shared_rows(key)
    return keys_drawn.astype(jnp.bfloat16)


def levels(own_key, shape, pieces, smallest, top_value):
    loudness, own = 1.0, jax.random.fold_in(own_key, 6)
    for dim, parts in pieces:
        heights = jnp.exp(jax.random.uniform(jax.random.fold_in(own, dim), (parts,), jnp.float32, smallest / len(pieces), top_value / len(pieces)))
        loudness = loudness * jnp.repeat(heights, shape[dim] // parts).reshape([-1 if axis == dim else 1 for axis in range(len(shape))])
    return loudness


def length_profile(number_of, total, most, slope):
    weights = [(1 << 20) // math.isqrt(standing ** slope) + 1 for standing in range(2, number_of + 1)]
    surplus, holding = total - most - (number_of - 1), [1] * (number_of - 1)
    while surplus > 0:
        candidates = [i for i in range(number_of - 1) if holding[i] < most]
        pool, remaining = sum([weights[i] for i in candidates]), surplus
        for i in candidates:
            more = min(most - holding[i], max(1, remaining * weights[i] // pool), surplus)
            holding[i] = holding[i] + more
            surplus = surplus - more
    return np.array([most] + holding)


def ragged_sizes(rng, number_of, total, reach, slope):
    if number_of == 2:
        one = jax.random.randint(rng, (), max(1, total - reach), min(reach, total - 1) + 1)
        return jnp.stack([one, total - one])
    lengths = jnp.asarray(length_profile(number_of, total, reach, slope), jnp.int32)
    pairs = (number_of - 1) // 2
    source_of, receiver = lengths[1:1 + 2 * pairs:2], lengths[2:2 + 2 * pairs:2]
    slack = jnp.minimum(source_of - 1, reach - receiver)
    shifted = jax.random.randint(jax.random.fold_in(rng, 1), (pairs,), 0, 1 << 20) % (slack + 1)
    lengths = lengths.at[1:1 + 2 * pairs:2].set(source_of - shifted).at[2:2 + 2 * pairs:2].set(receiver + shifted)
    return lengths[jax.random.permutation(jax.random.fold_in(rng, 2), number_of)]


def assign_block(own_key, own, number, rows, count, top, most, skew):
    order = jax.random.permutation(own_key, count)
    heavy_load, usual = portions_of(count, rows * top, most, skew, True), portions_of(count, rows * top, most, skew, False)
    places = jnp.arange(count)

    def named(sizes, turn):
        used = int((sizes > 0).sum())
        fixed = max(1, used // 4)
        passed = fixed + (places - fixed + turn * (used - fixed)) % max(1, count - fixed)
        return jnp.zeros((count,), jnp.int32).at[order[jnp.where(places < fixed, places, passed)]].set(jnp.asarray(sizes, jnp.int32))

    sizes = jnp.where(number % 4 == 0, named(heavy_load, number // 4), named(usual, number - number // 4 - 1))
    mixed = jax.random.permutation(jax.random.fold_in(own, 3), count)
    source_of, taker = mixed[0:count // 2 * 2:2], mixed[1:count // 2 * 2:2]
    slack = jnp.minimum(sizes[source_of] - 1, most - sizes[taker]) // 2
    slack = jnp.where((source_of == order[0]) | (taker == order[0]) | (sizes[taker] == 0), 0, jnp.maximum(slack, 0))
    passed = jax.random.randint(jax.random.fold_in(own, 4), (count // 2,), 0, 1 << 20) % (slack + 1)
    sizes = sizes.at[source_of].add(-passed).at[taker].add(passed)
    labels = jnp.searchsorted(jnp.cumsum(sizes), jnp.arange(rows * top), side="right").astype(jnp.int32)
    grid = labels.reshape(top, rows).T
    grid = grid[jax.random.permutation(jax.random.fold_in(own, 1), rows)]
    turn = jax.random.randint(jax.random.fold_in(own, 2), (rows, 1), 0, top)
    return jnp.take_along_axis(grid, (jnp.arange(top)[None, :] + turn) % top, axis=1)


def portions_of(count, total, bound, slope, full):
    portions = [(1 << 20) // math.isqrt(rank ** slope) + 1 for rank in range(1, count + 1)]
    largest = bound if full else min(bound, max(-(-total // count), total * portions[0] // sum(portions)))
    least = 1 if total - largest >= count - 1 else 0
    given, rest = [largest] + [least] * (count - 1), total - largest - least * (count - 1)
    while rest > 0:
        free = [i for i in range(1, count) if given[i] < largest] or [i for i in range(1, count) if given[i] < bound]
        mass, left = sum([portions[i] for i in free]), rest
        for i in free:
            extra = min(bound - given[i], max(1, left * portions[i] // mass), rest)
            given[i] = given[i] + extra
            rest = rest - extra
    return np.array(given)


def scatter_about(key, dims, scale, limit, pieces=(), held_as=jnp.bfloat16):
    values = scale * jax.random.normal(key, dims, jnp.float32)
    if pieces:
        values = values * levels(key, dims, pieces, -0.22, 0.18)
    return jnp.clip(values, -limit, limit).astype(held_as)


def setup_inputs(seed: int = 0, part: int = 0) -> dict:
    key_of = jax.random.split(jax.random.key(seed), 13)
    own_keys = jax.random.split(jax.random.fold_in(key_of[12], part), 13)
    queries = draw_queries(jax.random.fold_in(jax.random.fold_in(key_of[12], part), 71), part)
    key_rows = draw_key_rows(jax.random.fold_in(jax.random.fold_in(key_of[12], part), 71), part)
    value_rows = scatter_about(own_keys[2], (MB, TOKM, KVH * HD), 1.0, 5.0, ((1, 32),))
    residual = scatter_about(own_keys[3], (MB, TOKM, D), 0.5, 4.0, ((1, 32),))
    segment_ids = jnp.searchsorted(jnp.cumsum(ragged_sizes(own_keys[4], DOCS, TOKENS, DOC_MOST, 2)), jnp.arange(TOKENS), side="right").astype(jnp.int32)
    routes_keys = jax.random.split(jax.random.fold_in(own_keys[5], 1), MB * TOKM // TOKM_DEV)
    routes_turns = jax.random.permutation(jax.random.fold_in(own_keys[5], 3), MB * TOKM // TOKM_DEV)
    routes = jax.vmap(lambda own, number: assign_block(jax.random.fold_in(own_keys[5], 2), own, number, TOKM_DEV, EXPERTS, TOP, C, 2))(routes_keys, routes_turns).reshape((MB, TOKM, TOP))
    route_weights = jnp.clip(0.1 + 0.9 * jax.random.uniform(own_keys[6], (MB, TOKM, TOP), jnp.float32) ** levels(own_keys[6], (MB, TOKM, TOP), ((1, 32),), -0.2, 0.2), 0.1, 1.0)
    norm_gain = jnp.clip(1.0 + 0.1 * jax.random.normal(key_of[7], (D,), jnp.float32), 0.5, 1.5)
    norm_bias = scatter_about(key_of[8], (D,), 0.3, 3.0, (), jnp.float32)
    w_gate = scatter_about(key_of[9], (D, EXPERTS * FF), D ** -0.5, 0.09375, ((1, 32),))
    w_up = scatter_about(key_of[10], (D, EXPERTS * FF), D ** -0.5, 0.09375, ((1, 32),))
    w_down = scatter_about(key_of[11], (EXPERTS * FF, D), FF ** -0.5, 0.109375, ((0, 32),))
    return {"queries": queries, "key_rows": key_rows, "value_rows": value_rows, "residual": residual, "segment_ids": segment_ids, "routes": routes, "route_weights": route_weights, "norm_gain": norm_gain, "norm_bias": norm_bias, "w_gate": w_gate, "w_up": w_up, "w_down": w_down}


def attention_block(queries, key_rows, value_rows, segment_ids):
    group = HEADS // KVH
    scale = 1.0 / math.sqrt(HD)
    results = []
    for micro in range(MB):
        total_keys = (micro + 1) * TOKM
        key_all = key_rows[:micro + 1].reshape(total_keys, KVH, HD)
        value_all = value_rows[:micro + 1].reshape(total_keys, KVH, HD)
        query_now = queries[micro].reshape(TOKM, HEADS, HD)
        query_pos = micro * TOKM + jnp.arange(TOKM, dtype=jnp.int32)
        key_pos = jnp.arange(total_keys, dtype=jnp.int32)
        query_seg = segment_ids[micro * TOKM:(micro + 1) * TOKM]
        allowed = (segment_ids[:total_keys][None, :] == query_seg[:, None]) & (key_pos[None, :] <= query_pos[:, None])

        def one_head(head):
            query_head = lax.dynamic_index_in_dim(query_now, head, 1, keepdims=False)
            key_head = lax.dynamic_index_in_dim(key_all, head // group, 1, keepdims=False)
            value_head = lax.dynamic_index_in_dim(value_all, head // group, 1, keepdims=False)
            scores = jnp.dot(query_head, key_head.T, preferred_element_type=jnp.float32) * scale
            scores = jnp.where(allowed, scores, -1e+30)
            top = lax.optimization_barrier(jnp.max(scores, axis=1, keepdims=True))
            expo = jnp.exp(scores - top)
            probs = (expo / lax.optimization_barrier(jnp.sum(expo, axis=1, keepdims=True))).astype(jnp.bfloat16)
            return jnp.dot(probs, value_head, preferred_element_type=jnp.float32).astype(jnp.bfloat16)
        heads_out = lax.map(one_head, jnp.arange(HEADS, dtype=jnp.int32))
        results.append(jnp.transpose(heads_out, (1, 0, 2)).reshape(TOKM, HEADS * HD))
    return jnp.stack(results)

def reference(queries, key_rows, value_rows, residual, segment_ids, routes, route_weights, norm_gain, norm_bias, w_gate, w_up, w_down):
    attended = attention_block(queries, key_rows, value_rows, segment_ids)
    mixed = residual.astype(jnp.float32) + attended.astype(jnp.float32)
    center = mixed - lax.optimization_barrier(jnp.mean(mixed, axis=-1, keepdims=True))
    variance = lax.optimization_barrier(jnp.mean(center * center, axis=-1, keepdims=True))
    normed = (center / jnp.sqrt(variance + 1e-05) * norm_gain + norm_bias).astype(jnp.bfloat16)
    blocks = N_WIDE
    pairs = TOKM_DEV * TOP
    flat = routes.reshape(MB, blocks, pairs)
    onehot = (flat[..., None] == jnp.arange(EXPERTS, dtype=jnp.int32)).astype(jnp.int32)
    rank = jnp.cumsum(onehot, axis=2) - 1
    slot = lax.optimization_barrier(jnp.sum(onehot * rank, axis=-1))
    target = flat * C + slot
    chooser = (target[..., None] == jnp.arange(EXPERTS * C, dtype=jnp.int32)).astype(jnp.float32)
    chooser = chooser.reshape(MB, blocks, TOKM_DEV, TOP, EXPERTS * C).sum(axis=3)
    rows_in = normed.reshape(MB, blocks, TOKM_DEV, D).astype(jnp.float32)
    packed = jnp.einsum('mbte,mbtd->mbed', chooser, rows_in).astype(jnp.bfloat16)
    packed = packed.reshape(MB, blocks, EXPERTS, C, D)
    expert_rows = jnp.transpose(packed, (2, 0, 1, 3, 4)).reshape(EXPERTS, MB * blocks * C, D)

    def one_expert(args):
        expert, rows = args
        start = (expert * FF).astype(jnp.int32)
        gate = jnp.dot(rows, lax.dynamic_slice_in_dim(w_gate, start, FF, 1), preferred_element_type=jnp.float32)
        up = jnp.dot(rows, lax.dynamic_slice_in_dim(w_up, start, FF, 1), preferred_element_type=jnp.float32)
        hidden = (jax.nn.silu(gate) * up).astype(jnp.bfloat16)
        down = lax.dynamic_slice_in_dim(w_down, start, FF, 0)

        def add_block(block, total):
            begin = (block * FF_DEV).astype(jnp.int32)
            piece = jnp.dot(lax.dynamic_slice_in_dim(hidden, begin, FF_DEV, 1), lax.dynamic_slice_in_dim(down, begin, FF_DEV, 0), preferred_element_type=jnp.float32)
            rounded = lax.optimization_barrier(piece.astype(jnp.bfloat16))
            return total + rounded.astype(jnp.float32)
        return lax.fori_loop(0, FF // FF_DEV, add_block, jnp.zeros((rows.shape[0], D), jnp.float32))
    outputs = lax.map(one_expert, (jnp.arange(EXPERTS, dtype=jnp.int32), expert_rows))
    outputs = outputs.reshape(EXPERTS, MB, blocks, C, D)
    micro_idx = jnp.arange(MB, dtype=jnp.int32)[:, None, None]
    block_idx = jnp.arange(blocks, dtype=jnp.int32)[None, :, None]
    picked = outputs[flat, micro_idx, block_idx, slot]
    weighted = picked * route_weights.reshape(MB, blocks, pairs)[..., None]
    mixture = weighted.reshape(MB, blocks, TOKM_DEV, TOP, D).sum(axis=3).reshape(MB, TOKM, D)
    return (mixed + mixture).astype(jnp.bfloat16)
```

```python
import functools
import math

import jax
import jax.numpy as jnp
from jax import lax
from jax.experimental import pallas as pl
from jax.experimental.pallas import tpu as pltpu
from jax.sharding import PartitionSpec as P

HEADS = 32
KVH = 8
HD = 128
EXPERTS = 16
TOP = 2
C = 5


def passed_along(x, axis, by):
    length = lax.axis_size(axis)
    return lax.ppermute(x, axis, [(i, (i + by) % length) for i in range(length)])


def slot_targets(flat):
    onehot = (flat[..., None] == jnp.arange(EXPERTS, dtype=jnp.int32)).astype(jnp.int32)
    rank = jnp.cumsum(onehot, axis=-2) - 1
    slot = jnp.sum(onehot * rank, axis=-1)
    return flat * C + slot


UNITS_MOST = 400
VMEM_BYTES = 48 * 1024 * 1024
VMEM_MOST = 63 * 1024 * 1024


def tile_of(size):
    fits = [t for t in range(16, UNITS_MOST + 1, 16) if size % t == 0]
    return fits[-1] if fits else size


def expert_kernel(parts, *refs):
    row_refs = refs[:parts]
    gate_ref, up_ref, down_ref = refs[parts : parts + 3]
    out_refs = refs[parts + 3 : 2 * parts + 3]
    total = refs[2 * parts + 3]
    step = pl.program_id(0)
    last = pl.num_programs(0) - 1
    by_rows = (((1,), (1,)), ((), ()))
    rows = jnp.concatenate([ref[...] for ref in row_refs], axis=0)
    gate = lax.dot_general(rows, gate_ref[...], by_rows, preferred_element_type=jnp.float32)
    upward = lax.dot_general(rows, up_ref[...], by_rows, preferred_element_type=jnp.float32)
    hidden = (gate / (1.0 + jnp.exp(-gate)) * upward).astype(jnp.bfloat16)
    count = rows.shape[0] // parts
    added = jnp.dot(hidden, down_ref[...], preferred_element_type=jnp.float32)

    @pl.when(step == 0)
    def _():
        total[...] = added

    @pl.when(step > 0)
    def _():
        total[...] += added

    @pl.when(step == last)
    def _():
        for part in range(parts):
            block = total[part * count : (part + 1) * count, :]
            out_refs[part][...] = block.astype(jnp.bfloat16)


def compute_expert(row_parts, w_gate, w_up, w_down):
    parts = len(row_parts)
    count, width = row_parts[0].shape
    units = w_gate.shape[1]
    tile = tile_of(units)
    total = parts * count
    row_spec = pl.BlockSpec((count, width), lambda i: (0, 0))
    weight_spec = pl.BlockSpec((tile, width), lambda i: (i, 0))
    return pl.pallas_call(
        functools.partial(expert_kernel, parts),
        grid=(units // tile,),
        in_specs=[row_spec] * parts + [weight_spec] * 3,
        out_specs=[row_spec] * parts,
        out_shape=[jax.ShapeDtypeStruct((count, width), jnp.bfloat16)] * parts,
        scratch_shapes=[pltpu.VMEM((total, width), jnp.float32)],
        compiler_params=pltpu.CompilerParams(vmem_limit_bytes=VMEM_BYTES),
        cost_estimate=pl.CostEstimate(
            flops=6 * total * width * units,
            bytes_accessed=6 * width * units + 4 * total * width,
            transcendentals=total * units,
        ),
        name="expert",
    )(*row_parts, w_gate.T, w_up.T, w_down)


def shards(
    queries,
    key_rows,
    value_rows,
    residual,
    segment_ids,
    routes,
    route_weights,
    norm_gain,
    norm_bias,
    w_gate,
    w_up,
    w_down,
):
    wide_count = lax.axis_size("wide")
    device_index = lax.axis_index("wide")
    micro_count, tok_local, width = queries.shape
    tokens_micro = tok_local * wide_count
    doc_longest = micro_count * tokens_micro // 32
    scale = 1.0 / math.sqrt(HD)
    reach = doc_longest // tok_local
    group = HEADS // KVH
    steps_back = list(range(reach, 0, -1))
    received = []
    for step in steps_back:
        received.append(passed_along((key_rows, value_rows), "wide", step))
    span = (reach + 1) * tok_local
    before = jnp.full((reach * tok_local,), -1, jnp.int32)
    segments = jnp.concatenate([before, segment_ids])
    key_place = jnp.arange(span, dtype=jnp.int32) - reach * tok_local
    causal = key_place[None, :] <= jnp.arange(tok_local, dtype=jnp.int32)[:, None]
    results = []
    for local_micro in range(micro_count):
        earlier = max(local_micro - 1, 0)
        key_parts = []
        value_parts = []
        for position, step in enumerate(steps_back):
            key_far, value_far = received[position]
            crossed = device_index < step
            key_parts.append(jnp.where(crossed, key_far[earlier], key_far[local_micro]))
            value_parts.append(jnp.where(crossed, value_far[earlier], value_far[local_micro]))
        key_parts.append(key_rows[local_micro])
        value_parts.append(value_rows[local_micro])
        window_keys = jnp.concatenate(key_parts, axis=0)
        window_values = jnp.concatenate(value_parts, axis=0)
        key_seg = lax.dynamic_slice(
            segments, (local_micro * tokens_micro + device_index * tok_local,), (span,)
        )
        query_seg = key_seg[reach * tok_local :]
        allowed = (key_seg[None, :] == query_seg[:, None]) & causal
        query_now = queries[local_micro].reshape(tok_local, KVH, group, HD)
        scores = (
            jnp.einsum(
                "tkgd,skd->kgts",
                query_now,
                window_keys.reshape(span, KVH, HD),
                preferred_element_type=jnp.float32,
            )
            * scale
        )
        scores = jnp.where(allowed[None, None], scores, -1e30)
        top = jnp.max(scores, axis=3, keepdims=True)
        expo = jnp.exp(scores - top)
        probs = (expo / jnp.sum(expo, axis=3, keepdims=True)).astype(jnp.bfloat16)
        result = jnp.einsum(
            "kgts,skd->tkgd",
            probs,
            window_values.reshape(span, KVH, HD),
            preferred_element_type=jnp.float32,
        ).astype(jnp.bfloat16)
        results.append(result.reshape(tok_local, width))
    team = wide_count // EXPERTS
    across = [[e * team + r for e in range(EXPERTS)] for r in range(team)]
    inside = [[e * team + r for r in range(team)] for e in range(EXPERTS)]
    swap = [(i, i ^ 1) for i in range(wide_count)]
    fold = (width // 128, 128)
    slots = EXPERTS * C

    def exchanged(x):
        sent = x.reshape(EXPERTS, C, *fold)
        return lax.all_to_all(sent, "wide", 0, 0, axis_index_groups=across, tiled=True)

    state = []
    for micro in range(micro_count):
        mixed = residual[micro].astype(jnp.float32) + results[micro].astype(jnp.float32)
        center = mixed - jnp.mean(mixed, axis=-1, keepdims=True)
        variance = jnp.mean(center * center, axis=-1, keepdims=True)
        normed = (center / jnp.sqrt(variance + 1e-05) * norm_gain + norm_bias).astype(
            jnp.bfloat16
        )
        target = slot_targets(routes[micro].reshape(tok_local * TOP)).reshape(tok_local, TOP)
        hits = target[..., None] == jnp.arange(slots, dtype=jnp.int32)
        chooser = jnp.any(hits, axis=1).astype(jnp.bfloat16)
        packed = jnp.einsum(
            "te,td->ed", chooser, normed, preferred_element_type=jnp.float32
        ).astype(jnp.bfloat16)
        state.append((mixed, hits, exchanged(packed).reshape(slots, *fold)))
    outputs = []
    for micro in range(micro_count):
        mixed, hits, landed = state[micro]
        if team == 2:
            other = lax.ppermute(landed, "wide", swap)
            pair = (landed.reshape(slots, width), other.reshape(slots, width))
            mine, theirs = compute_expert(pair, w_gate, w_up, w_down)
            theirs = lax.ppermute(theirs, "wide", swap)
            summed = mine.astype(jnp.float32) + theirs.astype(jnp.float32)
        else:
            rows = lax.all_gather(landed, "wide", axis_index_groups=inside, tiled=True)
            rows = rows.reshape(team * slots, width)
            (partial_value,) = compute_expert((rows,), w_gate, w_up, w_down)
            blocks = lax.all_to_all(
                partial_value.reshape(team, slots, *fold),
                "wide",
                0,
                0,
                axis_index_groups=inside,
                tiled=True,
            )
            summed = blocks.astype(jnp.float32).sum(axis=0).reshape(slots, width)
        returned = exchanged(summed.astype(jnp.bfloat16)).reshape(slots, width)
        shares = jnp.sum(jnp.where(hits, route_weights[micro][..., None], 0.0), axis=1)
        high = shares.astype(jnp.bfloat16)
        low = (shares - high.astype(jnp.float32)).astype(jnp.bfloat16)
        mixture = jnp.dot(high, returned, preferred_element_type=jnp.float32) + jnp.dot(
            low, returned, preferred_element_type=jnp.float32
        )
        outputs.append((mixed + mixture).astype(jnp.bfloat16))
    return jnp.stack(outputs)


MESH_ID = pl.DeviceIdType.MESH


def flipped(place, by, bits):
    total = 0
    for bit in range(bits):
        own = (place // (1 << bit)) % 2
        total = total + ((own + (by >> bit) % 2) % 2) * (1 << bit)
    return total


def column_of(row):
    size = row.shape[1]
    down = lax.broadcasted_iota(jnp.int32, (size, size), 0)
    across = lax.broadcasted_iota(jnp.int32, (size, size), 1)
    spread = jnp.broadcast_to(row, (size, size))
    return jnp.sum(jnp.where(down == across, spread, 0.0), axis=1, keepdims=True)


def layer_kernel(
    sizes,
    seg_ref,
    routes_ref,
    shares_ref,
    gain_ref,
    bias_ref,
    q_hbm,
    k_hbm,
    v_hbm,
    res_hbm,
    gate_hbm,
    up_hbm,
    down_hbm,
    out_ref,
    q_buf,
    k_win,
    v_win,
    res_buf,
    gate_buf,
    up_buf,
    down_buf,
    mixed,
    normed,
    fold,
    send_buf,
    mine_buf,
    theirs_buf,
    rows_buf,
    hidden,
    part_own,
    part_send,
    part_recv,
    ret_buf,
    ret_recv,
    load_sem,
    weight_sem,
    kv_send,
    kv_recv,
    out_send,
    out_recv,
    pass_send,
    pass_recv,
    part_ssem,
    part_rsem,
    ret_send,
    ret_rsem,
):
    count, micros, tok, width, reach = sizes
    chips = count // 2
    bits = chips.bit_length() - 1
    lanes = width // 128
    slots = EXPERTS * C
    block = C * lanes
    group = HEADS // KVH
    span = (reach + 1) * tok
    units = gate_hbm.shape[0]
    me = lax.axis_index("wide")
    chip = me // 2
    core = me % 2
    partner = chip * 2 + (1 - core)
    order = list(range(chips - 1, 0, -1))

    def peer(k):
        return flipped(chip, k, bits) * 2 + core

    def to(device):
        return dict(device_id={"wide": device}, device_id_type=MESH_ID)

    loads = [
        pltpu.make_async_copy(q_hbm, q_buf, load_sem.at[0]),
        pltpu.make_async_copy(res_hbm, res_buf, load_sem.at[1]),
    ]
    for m in range(micros):
        own = pl.ds(reach * tok, tok)
        loads.append(pltpu.make_async_copy(k_hbm.at[m], k_win.at[m, own], load_sem.at[2 + 2 * m]))
        loads.append(pltpu.make_async_copy(v_hbm.at[m], v_win.at[m, own], load_sem.at[3 + 2 * m]))
    for load in loads:
        load.start()

    barrier = pltpu.get_barrier_semaphore()

    def greet(step, carry):
        pl.semaphore_signal(barrier, inc=1, **to((me + step) % count))
        return carry

    lax.fori_loop(1, count, greet, 0)
    pl.semaphore_wait(barrier, count - 1)

    kv_copies = {}
    for m in range(micros):
        for step in range(1, reach + 1):
            crossed = (me + step) // count
            source = (m + micros - crossed) % micros
            window = pl.ds((reach - step) * tok, tok)
            target = (me + step) % count
            for which, (far, win) in enumerate(((k_hbm, k_win), (v_hbm, v_win))):
                copy = pltpu.make_async_remote_copy(
                    far.at[source],
                    win.at[m, window],
                    kv_send.at[m, step - 1, which],
                    kv_recv.at[m, step - 1, which],
                    **to(target),
                )
                copy.start()
                kv_copies[m, step, which] = copy

    weight_loads = [
        pltpu.make_async_copy(far, near, weight_sem.at[i])
        for i, (far, near) in enumerate(
            ((gate_hbm, gate_buf), (up_hbm, up_buf), (down_hbm, down_buf))
        )
    ]
    for load in weight_loads:
        load.start()

    def allowed_of(m):
        start = m * tok * count + me * tok - reach * tok
        rows = seg_ref.shape[0]
        first = (start + rows * 128) // 128
        both = jnp.concatenate(
            [seg_ref[pl.ds(first % rows, 1), :], seg_ref[pl.ds((first + 1) % rows, 1), :]],
            axis=1,
        )
        shift = (start + rows * 128) % 128
        seg = both[:, 0:span]
        for skip in range(tok, 128, tok):
            picked = (jnp.zeros((1, span), jnp.int32) + shift) == skip
            seg = jnp.where(picked, both[:, skip : skip + span], seg)
        seg = seg.astype(jnp.float32)
        query_seg = column_of(seg[:, reach * tok :])
        place = lax.broadcasted_iota(jnp.int32, (tok, span), 1)
        now = lax.broadcasted_iota(jnp.int32, (tok, span), 0)
        fits = jnp.broadcast_to(seg, (tok, span)) == jnp.broadcast_to(query_seg, (tok, span))
        fits = fits & (place <= now + reach * tok) & (place + start >= 0)
        return jnp.concatenate([jnp.where(fits, 1.0, 0.0)] * group, axis=0)

    def slot_maps(m):
        names = routes_ref[m].astype(jnp.float32)
        row_names = [names[i : i + 1, :] for i in range(TOP)]
        col_names = [column_of(row) for row in row_names]
        weights = [column_of(shares_ref[m][i : i + 1, :]) for i in range(TOP)]
        before = lax.broadcasted_iota(jnp.int32, (tok, tok), 0)
        after = lax.broadcasted_iota(jnp.int32, (tok, tok), 1)

        def slot_rows(i):
            total = jnp.zeros((tok, tok), jnp.float32)
            for other in range(TOP):
                same = (col_names[other] == row_names[i]) & (before < after)
                total = total + jnp.where(same, 1.0, 0.0)
            return jnp.sum(total, axis=0, keepdims=True)

        def slot_cols(i):
            total = jnp.zeros((tok, tok), jnp.float32)
            for other in range(TOP):
                same = (row_names[other] == col_names[i]) & (after < before)
                total = total + jnp.where(same, 1.0, 0.0)
            return jnp.sum(total, axis=1, keepdims=True)

        def places(shape, axis):
            at = lax.broadcasted_iota(jnp.int32, shape, axis)
            turn = jnp.zeros(shape, jnp.int32)
            for k in range(1, EXPERTS):
                turn = turn + jnp.where(at >= k * C, 1, 0)
            expert = jnp.bitwise_xor(turn, jnp.zeros(shape, jnp.int32) + chip)
            return expert.astype(jnp.float32), (at - turn * C).astype(jnp.float32)

        expert, slot = places((slots, tok), 0)
        chooser = jnp.zeros((slots, tok), jnp.float32)
        for i in range(TOP):
            chooser = chooser + jnp.where(
                (expert == row_names[i]) & (slot == slot_rows(i)), 1.0, 0.0
            )
        expert, slot = places((tok, slots), 1)
        parts = jnp.zeros((tok, slots), jnp.float32)
        for i in range(TOP):
            parts = parts + jnp.where(
                (expert == col_names[i]) & (slot == slot_cols(i)), weights[i], 0.0
            )
        high = parts.astype(jnp.bfloat16)
        low = (parts - high.astype(jnp.float32)).astype(jnp.bfloat16)
        return chooser.astype(jnp.bfloat16), jnp.concatenate([high, low], axis=0)

    by_rows = (((1,), (1,)), ((), ()))
    scale = 1.0 / math.sqrt(HD)

    def attend(m, allowed):
        for head in range(KVH):
            cols = slice(head * HD, (head + 1) * HD)
            first = head * group
            queries = jnp.concatenate(
                [q_buf[m, :, (first + g) * HD : (first + g + 1) * HD] for g in range(group)],
                axis=0,
            )
            scores = lax.dot_general(
                queries, k_win[m, :, cols], by_rows, preferred_element_type=jnp.float32
            )
            scores = jnp.where(allowed > 0.5, scores * scale, -1e30)
            expo = jnp.exp(scores - jnp.max(scores, axis=1, keepdims=True))
            probs = (expo / jnp.sum(expo, axis=1, keepdims=True)).astype(jnp.bfloat16)
            result = jnp.dot(probs, v_win[m, :, cols], preferred_element_type=jnp.float32)
            result = result.astype(jnp.bfloat16).astype(jnp.float32)
            for g in range(group):
                at = slice((first + g) * HD, (first + g + 1) * HD)
                mixed[m, :, at] = (
                    res_buf[m, :, at].astype(jnp.float32) + result[g * tok : (g + 1) * tok, :]
                )

    def normalize(m):
        values = mixed[m]
        center = values - jnp.mean(values, axis=1, keepdims=True)
        variance = jnp.mean(center * center, axis=1, keepdims=True)
        scaled = center * (1.0 / jnp.sqrt(variance + 1e-05))
        normed[...] = (scaled * gain_ref[...] + bias_ref[...]).astype(jnp.bfloat16)

    chunk = min(512, width)
    per_chunk = chunk // 128

    def pack(m, chooser):
        for j in range(width // chunk):
            packed = jnp.dot(
                chooser, normed[:, j * chunk : (j + 1) * chunk], preferred_element_type=jnp.float32
            )
            for i in range(per_chunk):
                fold[pl.ds(j * per_chunk + i, slots, stride=lanes), :] = packed[
                    :, i * 128 : (i + 1) * 128
                ]
        for k in order + [0]:
            send_buf[m, k] = fold[k * block : (k + 1) * block, :].astype(jnp.bfloat16)

    def exchange(m, k, source, target, ssem, rsem, device):
        return pltpu.make_async_remote_copy(
            source.at[m, k], target.at[m, k], ssem.at[m, k], rsem.at[m, k], **to(device)
        )

    def sent(m, k):
        return exchange(m, k, send_buf, mine_buf, out_send, out_recv, peer(k))

    def passed(m, k):
        source = mine_buf if k else send_buf
        return exchange(m, k, source, theirs_buf, pass_send, pass_recv, partner)

    def returned(m, k):
        return exchange(m, k, ret_buf, ret_recv, ret_send, ret_rsem, peer(k))

    def swapped(m, j):
        return exchange(m, j, part_send, part_recv, part_ssem, part_rsem, partner)

    def first_half(m, allowed, chooser):
        for step in range(1, reach + 1):
            for which in range(2):
                kv_copies[m, step, which].wait_recv()
        if m == 0:
            for load in loads:
                load.wait()
        attend(m, allowed)
        normalize(m)
        pack(m, chooser)
        for k in order:
            sent(m, k).start()
        passed(m, 0).start()

    def lay_rows(at):
        for j in range(lanes):
            rows_buf[at : at + slots, j * 128 : (j + 1) * 128] = fold[
                pl.ds(j, slots, stride=lanes), :
            ].astype(jnp.bfloat16)

    def gather_rows(m):
        fold[0:block, :] = send_buf[m, 0].astype(jnp.float32)
        for k in order:
            sent(m, k).wait_recv()
            passed(m, k).start()
            fold[k * block : (k + 1) * block, :] = mine_buf[m, k].astype(jnp.float32)
        lay_rows(0)
        for k in [0] + order:
            passed(m, k).wait_recv()
            fold[k * block : (k + 1) * block, :] = theirs_buf[m, k].astype(jnp.float32)
        lay_rows(slots)

    tile = 256
    whole_tiles = units // tile

    def hidden_tile(start, size):
        rows = rows_buf[...]
        at = pl.ds(start, size)
        gate = lax.dot_general(
            rows, gate_buf[at, :], by_rows, preferred_element_type=jnp.float32
        )
        upward = lax.dot_general(
            rows, up_buf[at, :], by_rows, preferred_element_type=jnp.float32
        )
        hidden[:, at] = (gate / (1.0 + jnp.exp(-gate)) * upward).astype(jnp.bfloat16)

    def experts(m):
        def hidden_step(i, carry):
            hidden_tile(pl.multiple_of(i * tile, tile), tile)
            return carry

        lax.fori_loop(0, whole_tiles, hidden_step, 0)
        if units % tile:
            hidden_tile(whole_tiles * tile, units % tile)

        def down_step(j, carry):
            at = pl.ds(pl.multiple_of(j * chunk, chunk), chunk)
            added = jnp.dot(hidden[...], down_buf[:, at], preferred_element_type=jnp.float32)
            added = added.astype(jnp.bfloat16)
            part_own[j] = added[0:slots, :]
            part_send[m, j] = added[slots : 2 * slots, :]
            swapped(m, j).start()
            return carry

        lax.fori_loop(0, width // chunk, down_step, 0)

    def give_back(m):
        for j in range(width // chunk):
            swapped(m, j).wait_recv()
            total = part_own[j].astype(jnp.float32) + part_recv[m, j].astype(jnp.float32)
            for i in range(per_chunk):
                fold[pl.ds(j * per_chunk + i, slots, stride=lanes), :] = total[
                    :, i * 128 : (i + 1) * 128
                ]
        for k in order + [0]:
            ret_buf[m, k] = fold[k * block : (k + 1) * block, :].astype(jnp.bfloat16)
        for k in order:
            returned(m, k).start()

    def combine(m, parts):
        fold[0:block, :] = ret_buf[m, 0].astype(jnp.float32)
        for k in order:
            returned(m, k).wait_recv()
            fold[k * block : (k + 1) * block, :] = ret_recv[m, k].astype(jnp.float32)
        for j in range(width // chunk):
            pieces = [
                fold[pl.ds(j * per_chunk + i, slots, stride=lanes), :].astype(jnp.bfloat16)
                for i in range(per_chunk)
            ]
            both = jnp.dot(
                parts, jnp.concatenate(pieces, axis=1), preferred_element_type=jnp.float32
            )
            at = slice(j * chunk, (j + 1) * chunk)
            out_ref[m, :, at] = (mixed[m, :, at] + (both[0:tok] + both[tok : 2 * tok])).astype(
                jnp.bfloat16
            )

    masks = [allowed_of(m) for m in range(micros)]
    maps = [slot_maps(m) for m in range(micros)]
    for m in range(micros):
        first_half(m, masks[m], maps[m][0])
    for m in range(micros):
        gather_rows(m)
        if m == 0:
            for load in weight_loads:
                load.wait()
        experts(m)
        give_back(m)
    for m in range(micros):
        combine(m, maps[m][1])
    for m in range(micros):
        for step in range(1, reach + 1):
            for which in range(2):
                kv_copies[m, step, which].wait_send()
        for k in order:
            sent(m, k).wait_send()
            returned(m, k).wait_send()
        for k in [0] + order:
            passed(m, k).wait_send()
        for j in range(width // chunk):
            swapped(m, j).wait_send()


def whole_layer(
    queries,
    key_rows,
    value_rows,
    residual,
    segment_ids,
    routes,
    route_weights,
    norm_gain,
    norm_bias,
    w_gate,
    w_up,
    w_down,
):
    count = lax.axis_size("wide")
    micros, tok, width = queries.shape
    reach = micros * tok * count // 32 // tok
    kv_width = key_rows.shape[2]
    units = w_gate.shape[1]
    chips = count // 2
    slots = EXPERTS * C
    lanes = width // 128
    block = C * lanes
    span = (reach + 1) * tok
    chunk = min(512, width)
    chunks = width // chunk
    near = pl.BlockSpec(memory_space=pltpu.VMEM)
    far = pl.BlockSpec(memory_space=pl.ANY)
    half = jnp.bfloat16
    full = jnp.float32
    exchange = pltpu.VMEM((micros, chips, block, 128), half)
    weight = pltpu.VMEM((units, width), half)
    dma = pltpu.SemaphoreType.DMA
    scratch = [
        pltpu.VMEM((micros, tok, width), half),
        pltpu.VMEM((micros, span, kv_width), half),
        pltpu.VMEM((micros, span, kv_width), half),
        pltpu.VMEM((micros, tok, width), half),
        weight,
        weight,
        weight,
        pltpu.VMEM((micros, tok, width), full),
        pltpu.VMEM((tok, width), half),
        pltpu.VMEM((slots * lanes, 128), full),
        exchange,
        exchange,
        exchange,
        pltpu.VMEM((2 * slots, width), half),
        pltpu.VMEM((2 * slots, units), half),
        pltpu.VMEM((chunks, slots, chunk), half),
        pltpu.VMEM((micros, chunks, slots, chunk), half),
        pltpu.VMEM((micros, chunks, slots, chunk), half),
        exchange,
        exchange,
        dma((2 + 2 * micros,)),
        dma((3,)),
        dma((micros, reach, 2)),
        dma((micros, reach, 2)),
        dma((micros, chips)),
        dma((micros, chips)),
        dma((micros, chips)),
        dma((micros, chips)),
        dma((micros, chunks)),
        dma((micros, chunks)),
        dma((micros, chips)),
        dma((micros, chips)),
    ]
    return pl.pallas_call(
        functools.partial(layer_kernel, (count, micros, tok, width, reach)),
        out_shape=jax.ShapeDtypeStruct((micros, tok, width), half),
        in_specs=[near] * 5 + [far] * 7,
        out_specs=near,
        scratch_shapes=scratch,
        compiler_params=pltpu.CompilerParams(
            collective_id=0, has_side_effects=True, vmem_limit_bytes=VMEM_MOST
        ),
        name="layer",
    )(
        segment_ids.reshape(-1, 128),
        jnp.transpose(routes, (0, 2, 1)),
        jnp.transpose(route_weights, (0, 2, 1)),
        norm_gain.reshape(1, width),
        norm_bias.reshape(1, width),
        queries,
        key_rows,
        value_rows,
        residual,
        w_gate.T,
        w_up.T,
        w_down,
    )


def solution(mesh):
    placed = (
        P("groups", "wide", None),
        P("groups", "wide", None),
        P("groups", "wide", None),
        P("groups", "wide", None),
        P("groups"),
        P("groups", "wide", None),
        P("groups", "wide", None),
        P(),
        P(),
        P(None, "wide"),
        P(None, "wide"),
        P("wide", None),
    )
    wide_count = mesh.shape["wide"]
    paired = wide_count == 2 * EXPERTS

    def layer(*args):
        return whole_layer(*args) if paired else shards(*args)

    return jax.shard_map(
        layer, mesh=mesh, in_specs=placed, out_specs=P("groups", "wide", None), check_vma=False
    )
```

```python
import functools
import math

import jax
import jax.numpy as jnp
from jax import lax
from jax.experimental import pallas as pl
from jax.experimental.pallas import tpu as pltpu
from jax.sharding import PartitionSpec as P

HEADS = 32
KVH = 8
HD = 128
EXPERTS = 16
TOP = 2
C = 5


def passed_along(x, axis, by):
    length = lax.axis_size(axis)
    return lax.ppermute(x, axis, [(i, (i + by) % length) for i in range(length)])


def slot_targets(flat):
    onehot = (flat[..., None] == jnp.arange(EXPERTS, dtype=jnp.int32)).astype(jnp.int32)
    rank = jnp.cumsum(onehot, axis=-2) - 1
    slot = jnp.sum(onehot * rank, axis=-1)
    return flat * C + slot


UNITS_MOST = 400
VMEM_BYTES = 48 * 1024 * 1024
VMEM_MOST = 56 * 1024 * 1024


def tile_of(size):
    fits = [t for t in range(16, UNITS_MOST + 1, 16) if size % t == 0]
    return fits[-1] if fits else size


def expert_kernel(parts, *refs):
    row_refs = refs[:parts]
    gate_ref, up_ref, down_ref = refs[parts : parts + 3]
    out_refs = refs[parts + 3 : 2 * parts + 3]
    total = refs[2 * parts + 3]
    step = pl.program_id(0)
    last = pl.num_programs(0) - 1
    by_rows = (((1,), (1,)), ((), ()))
    rows = jnp.concatenate([ref[...] for ref in row_refs], axis=0)
    gate = lax.dot_general(rows, gate_ref[...], by_rows, preferred_element_type=jnp.float32)
    upward = lax.dot_general(rows, up_ref[...], by_rows, preferred_element_type=jnp.float32)
    hidden = (gate / (1.0 + jnp.exp(-gate)) * upward).astype(jnp.bfloat16)
    count = rows.shape[0] // parts
    added = jnp.dot(hidden, down_ref[...], preferred_element_type=jnp.float32)

    @pl.when(step == 0)
    def _():
        total[...] = added

    @pl.when(step > 0)
    def _():
        total[...] += added

    @pl.when(step == last)
    def _():
        for part in range(parts):
            block = total[part * count : (part + 1) * count, :]
            out_refs[part][...] = block.astype(jnp.bfloat16)


def compute_expert(row_parts, w_gate, w_up, w_down):
    parts = len(row_parts)
    count, width = row_parts[0].shape
    units = w_gate.shape[1]
    tile = tile_of(units)
    total = parts * count
    row_spec = pl.BlockSpec((count, width), lambda i: (0, 0))
    weight_spec = pl.BlockSpec((tile, width), lambda i: (i, 0))
    return pl.pallas_call(
        functools.partial(expert_kernel, parts),
        grid=(units // tile,),
        in_specs=[row_spec] * parts + [weight_spec] * 3,
        out_specs=[row_spec] * parts,
        out_shape=[jax.ShapeDtypeStruct((count, width), jnp.bfloat16)] * parts,
        scratch_shapes=[pltpu.VMEM((total, width), jnp.float32)],
        compiler_params=pltpu.CompilerParams(vmem_limit_bytes=VMEM_BYTES),
        cost_estimate=pl.CostEstimate(
            flops=6 * total * width * units,
            bytes_accessed=6 * width * units + 4 * total * width,
            transcendentals=total * units,
        ),
        name="expert",
    )(*row_parts, w_gate.T, w_up.T, w_down)


def shards(
    queries,
    key_rows,
    value_rows,
    residual,
    segment_ids,
    routes,
    route_weights,
    norm_gain,
    norm_bias,
    w_gate,
    w_up,
    w_down,
):
    wide_count = lax.axis_size("wide")
    device_index = lax.axis_index("wide")
    micro_count, tok_local, width = queries.shape
    tokens_micro = tok_local * wide_count
    doc_longest = micro_count * tokens_micro // 32
    scale = 1.0 / math.sqrt(HD)
    reach = doc_longest // tok_local
    group = HEADS // KVH
    steps_back = list(range(reach, 0, -1))
    received = []
    for step in steps_back:
        received.append(passed_along((key_rows, value_rows), "wide", step))
    span = (reach + 1) * tok_local
    before = jnp.full((reach * tok_local,), -1, jnp.int32)
    segments = jnp.concatenate([before, segment_ids])
    key_place = jnp.arange(span, dtype=jnp.int32) - reach * tok_local
    causal = key_place[None, :] <= jnp.arange(tok_local, dtype=jnp.int32)[:, None]
    results = []
    for local_micro in range(micro_count):
        earlier = max(local_micro - 1, 0)
        key_parts = []
        value_parts = []
        for position, step in enumerate(steps_back):
            key_far, value_far = received[position]
            crossed = device_index < step
            key_parts.append(jnp.where(crossed, key_far[earlier], key_far[local_micro]))
            value_parts.append(jnp.where(crossed, value_far[earlier], value_far[local_micro]))
        key_parts.append(key_rows[local_micro])
        value_parts.append(value_rows[local_micro])
        window_keys = jnp.concatenate(key_parts, axis=0)
        window_values = jnp.concatenate(value_parts, axis=0)
        key_seg = lax.dynamic_slice(
            segments, (local_micro * tokens_micro + device_index * tok_local,), (span,)
        )
        query_seg = key_seg[reach * tok_local :]
        allowed = (key_seg[None, :] == query_seg[:, None]) & causal
        query_now = queries[local_micro].reshape(tok_local, KVH, group, HD)
        scores = (
            jnp.einsum(
                "tkgd,skd->kgts",
                query_now,
                window_keys.reshape(span, KVH, HD),
                preferred_element_type=jnp.float32,
            )
            * scale
        )
        scores = jnp.where(allowed[None, None], scores, -1e30)
        top = jnp.max(scores, axis=3, keepdims=True)
        expo = jnp.exp(scores - top)
        probs = (expo / jnp.sum(expo, axis=3, keepdims=True)).astype(jnp.bfloat16)
        result = jnp.einsum(
            "kgts,skd->tkgd",
            probs,
            window_values.reshape(span, KVH, HD),
            preferred_element_type=jnp.float32,
        ).astype(jnp.bfloat16)
        results.append(result.reshape(tok_local, width))
    team = wide_count // EXPERTS
    across = [[e * team + r for e in range(EXPERTS)] for r in range(team)]
    inside = [[e * team + r for r in range(team)] for e in range(EXPERTS)]
    swap = [(i, i ^ 1) for i in range(wide_count)]
    fold = (width // 128, 128)
    slots = EXPERTS * C

    def exchanged(x):
        sent = x.reshape(EXPERTS, C, *fold)
        return lax.all_to_all(sent, "wide", 0, 0, axis_index_groups=across, tiled=True)

    state = []
    for micro in range(micro_count):
        mixed = residual[micro].astype(jnp.float32) + results[micro].astype(jnp.float32)
        center = mixed - jnp.mean(mixed, axis=-1, keepdims=True)
        variance = jnp.mean(center * center, axis=-1, keepdims=True)
        normed = (center / jnp.sqrt(variance + 1e-05) * norm_gain + norm_bias).astype(
            jnp.bfloat16
        )
        target = slot_targets(routes[micro].reshape(tok_local * TOP)).reshape(tok_local, TOP)
        hits = target[..., None] == jnp.arange(slots, dtype=jnp.int32)
        chooser = jnp.any(hits, axis=1).astype(jnp.bfloat16)
        packed = jnp.einsum(
            "te,td->ed", chooser, normed, preferred_element_type=jnp.float32
        ).astype(jnp.bfloat16)
        state.append((mixed, hits, exchanged(packed).reshape(slots, *fold)))
    outputs = []
    for micro in range(micro_count):
        mixed, hits, landed = state[micro]
        if team == 2:
            other = lax.ppermute(landed, "wide", swap)
            pair = (landed.reshape(slots, width), other.reshape(slots, width))
            mine, theirs = compute_expert(pair, w_gate, w_up, w_down)
            theirs = lax.ppermute(theirs, "wide", swap)
            summed = mine.astype(jnp.float32) + theirs.astype(jnp.float32)
        else:
            rows = lax.all_gather(landed, "wide", axis_index_groups=inside, tiled=True)
            rows = rows.reshape(team * slots, width)
            (partial_value,) = compute_expert((rows,), w_gate, w_up, w_down)
            blocks = lax.all_to_all(
                partial_value.reshape(team, slots, *fold),
                "wide",
                0,
                0,
                axis_index_groups=inside,
                tiled=True,
            )
            summed = blocks.astype(jnp.float32).sum(axis=0).reshape(slots, width)
        returned = exchanged(summed.astype(jnp.bfloat16)).reshape(slots, width)
        shares = jnp.sum(jnp.where(hits, route_weights[micro][..., None], 0.0), axis=1)
        high = shares.astype(jnp.bfloat16)
        low = (shares - high.astype(jnp.float32)).astype(jnp.bfloat16)
        mixture = jnp.dot(high, returned, preferred_element_type=jnp.float32) + jnp.dot(
            low, returned, preferred_element_type=jnp.float32
        )
        outputs.append((mixed + mixture).astype(jnp.bfloat16))
    return jnp.stack(outputs)


MESH_ID = pl.DeviceIdType.MESH


def flipped(place, by, bits):
    total = 0
    for bit in range(bits):
        own = (place // (1 << bit)) % 2
        total = total + ((own + (by >> bit) % 2) % 2) * (1 << bit)
    return total


def column_of(row):
    size = row.shape[1]
    down = lax.broadcasted_iota(jnp.int32, (size, size), 0)
    across = lax.broadcasted_iota(jnp.int32, (size, size), 1)
    spread = jnp.broadcast_to(row, (size, size))
    return jnp.sum(jnp.where(down == across, spread, 0.0), axis=1, keepdims=True)


def layer_kernel(
    sizes,
    seg_ref,
    routes_ref,
    shares_ref,
    gain_ref,
    bias_ref,
    q_hbm,
    k_hbm,
    v_hbm,
    res_hbm,
    gate_hbm,
    up_hbm,
    down_hbm,
    out_ref,
    q_buf,
    k_win,
    v_win,
    res_buf,
    gate_buf,
    up_buf,
    down_buf,
    mixed,
    normed,
    fold,
    send_buf,
    mine_buf,
    theirs_buf,
    rows_buf,
    hidden,
    part_own,
    part_send,
    part_recv,
    ret_buf,
    ret_recv,
    load_sem,
    weight_sem,
    kv_send,
    kv_recv,
    out_send,
    out_recv,
    pass_send,
    pass_recv,
    part_ssem,
    part_rsem,
    ret_send,
    ret_rsem,
):
    count, micros, tok, width, reach = sizes
    chips = count // 2
    bits = chips.bit_length() - 1
    lanes = width // 128
    slots = EXPERTS * C
    block = C * lanes
    group = HEADS // KVH
    span = (reach + 1) * tok
    units = gate_hbm.shape[0]
    me = lax.axis_index("wide")
    chip = me // 2
    core = me % 2
    partner = chip * 2 + (1 - core)
    order = list(range(chips - 1, 0, -1))

    def peer(k):
        return flipped(chip, k, bits) * 2 + core

    def to(device):
        return dict(device_id={"wide": device}, device_id_type=MESH_ID)

    loads = [
        pltpu.make_async_copy(q_hbm, q_buf, load_sem.at[0]),
        pltpu.make_async_copy(res_hbm, res_buf, load_sem.at[1]),
    ]
    for m in range(micros):
        own = pl.ds(reach * tok, tok)
        loads.append(pltpu.make_async_copy(k_hbm.at[m], k_win.at[m, own], load_sem.at[2 + 2 * m]))
        loads.append(pltpu.make_async_copy(v_hbm.at[m], v_win.at[m, own], load_sem.at[3 + 2 * m]))
    for load in loads:
        load.start()

    barrier = pltpu.get_barrier_semaphore()

    def greet(step, carry):
        pl.semaphore_signal(barrier, inc=1, **to((me + step) % count))
        return carry

    lax.fori_loop(1, count, greet, 0)

    def allowed_of(m):
        start = m * tok * count + me * tok - reach * tok
        rows = seg_ref.shape[0]
        first = (start + rows * 128) // 128
        both = jnp.concatenate(
            [seg_ref[pl.ds(first % rows, 1), :], seg_ref[pl.ds((first + 1) % rows, 1), :]],
            axis=1,
        )
        shift = (start + rows * 128) % 128
        seg = both[:, 0:span]
        for skip in range(tok, 128, tok):
            picked = (jnp.zeros((1, span), jnp.int32) + shift) == skip
            seg = jnp.where(picked, both[:, skip : skip + span], seg)
        seg = seg.astype(jnp.float32)
        query_seg = column_of(seg[:, reach * tok :])
        place = lax.broadcasted_iota(jnp.int32, (tok, span), 1)
        now = lax.broadcasted_iota(jnp.int32, (tok, span), 0)
        fits = jnp.broadcast_to(seg, (tok, span)) == jnp.broadcast_to(query_seg, (tok, span))
        fits = fits & (place <= now + reach * tok) & (place + start >= 0)
        return jnp.concatenate([jnp.where(fits, 1.0, 0.0)] * group, axis=0)

    def slot_maps(m):
        names = routes_ref[m].astype(jnp.float32)
        row_names = [names[i : i + 1, :] for i in range(TOP)]
        col_names = [column_of(row) for row in row_names]
        weights = [column_of(shares_ref[m][i : i + 1, :]) for i in range(TOP)]
        before = lax.broadcasted_iota(jnp.int32, (tok, tok), 0)
        after = lax.broadcasted_iota(jnp.int32, (tok, tok), 1)

        def slot_rows(i):
            total = jnp.zeros((tok, tok), jnp.float32)
            for other in range(TOP):
                same = (col_names[other] == row_names[i]) & (before < after)
                total = total + jnp.where(same, 1.0, 0.0)
            return jnp.sum(total, axis=0, keepdims=True)

        def slot_cols(i):
            total = jnp.zeros((tok, tok), jnp.float32)
            for other in range(TOP):
                same = (row_names[other] == col_names[i]) & (after < before)
                total = total + jnp.where(same, 1.0, 0.0)
            return jnp.sum(total, axis=1, keepdims=True)

        def places(shape, axis):
            at = lax.broadcasted_iota(jnp.int32, shape, axis)
            turn = jnp.zeros(shape, jnp.int32)
            for k in range(1, EXPERTS):
                turn = turn + jnp.where(at >= k * C, 1, 0)
            expert = jnp.bitwise_xor(turn, jnp.zeros(shape, jnp.int32) + chip)
            return expert.astype(jnp.float32), (at - turn * C).astype(jnp.float32)

        expert, slot = places((slots, tok), 0)
        chooser = jnp.zeros((slots, tok), jnp.float32)
        for i in range(TOP):
            chooser = chooser + jnp.where(
                (expert == row_names[i]) & (slot == slot_rows(i)), 1.0, 0.0
            )
        expert, slot = places((tok, slots), 1)
        parts = jnp.zeros((tok, slots), jnp.float32)
        for i in range(TOP):
            parts = parts + jnp.where(
                (expert == col_names[i]) & (slot == slot_cols(i)), weights[i], 0.0
            )
        high = parts.astype(jnp.bfloat16)
        low = (parts - high.astype(jnp.float32)).astype(jnp.bfloat16)
        return chooser.astype(jnp.bfloat16), jnp.concatenate([high, low], axis=0)

    masks = [allowed_of(m) for m in range(micros)]
    maps = [slot_maps(m) for m in range(micros)]
    pl.semaphore_wait(barrier, count - 1)

    kv_copies = {}
    for m in range(micros):
        for step in range(1, reach + 1):
            crossed = (me + step) // count
            source = (m + micros - crossed) % micros
            window = pl.ds((reach - step) * tok, tok)
            target = (me + step) % count
            for which, (far, win) in enumerate(((k_hbm, k_win), (v_hbm, v_win))):
                copy = pltpu.make_async_remote_copy(
                    far.at[source],
                    win.at[m, window],
                    kv_send.at[m, step - 1, which],
                    kv_recv.at[m, step - 1, which],
                    **to(target),
                )
                copy.start()
                kv_copies[m, step, which] = copy

    weight_loads = [
        pltpu.make_async_copy(far, near, weight_sem.at[i])
        for i, (far, near) in enumerate(
            ((gate_hbm, gate_buf), (up_hbm, up_buf), (down_hbm, down_buf))
        )
    ]
    for load in weight_loads:
        load.start()

    by_rows = (((1,), (1,)), ((), ()))
    scale = 1.0 / math.sqrt(HD)

    def attend(m, allowed):
        together = KVH // 2
        for start in range(0, KVH, together):
            heads = range(start, start + together)
            cols = [slice(head * HD, (head + 1) * HD) for head in heads]
            scores = []
            for head, at in zip(heads, cols):
                queries = [
                    q_buf[m, :, (head * group + g) * HD : (head * group + g + 1) * HD]
                    for g in range(group)
                ]
                scores.append(
                    lax.dot_general(
                        jnp.concatenate(queries, axis=0),
                        k_win[m, :, at],
                        by_rows,
                        preferred_element_type=jnp.float32,
                    )
                )
            scores = [jnp.where(allowed > 0.5, score * scale, -1e30) for score in scores]
            tops = [jnp.max(score, axis=1, keepdims=True) for score in scores]
            expos = [jnp.exp(score - top) for score, top in zip(scores, tops)]
            sums = [jnp.sum(expo, axis=1, keepdims=True) for expo in expos]
            probs = [(expo / total).astype(jnp.bfloat16) for expo, total in zip(expos, sums)]
            results = [
                jnp.dot(prob, v_win[m, :, at], preferred_element_type=jnp.float32)
                for prob, at in zip(probs, cols)
            ]
            for head, result in zip(heads, results):
                result = result.astype(jnp.bfloat16).astype(jnp.float32)
                for g in range(group):
                    at = slice((head * group + g) * HD, (head * group + g + 1) * HD)
                    mixed[m, :, at] = (
                        res_buf[m, :, at].astype(jnp.float32) + result[g * tok : (g + 1) * tok, :]
                    )

    def normalize(m):
        values = mixed[m]
        center = values - jnp.mean(values, axis=1, keepdims=True)
        variance = jnp.mean(center * center, axis=1, keepdims=True)
        scaled = center * (1.0 / jnp.sqrt(variance + 1e-05))
        normed[...] = (scaled * gain_ref[...] + bias_ref[...]).astype(jnp.bfloat16)

    chunk = min(1024, width)
    per_chunk = chunk // 128

    def pack(m, chooser):
        for j in range(width // chunk):
            packed = jnp.dot(
                chooser, normed[:, j * chunk : (j + 1) * chunk], preferred_element_type=jnp.float32
            )
            for i in range(per_chunk):
                fold[pl.ds(j * per_chunk + i, slots, stride=lanes), :] = packed[
                    :, i * 128 : (i + 1) * 128
                ]
        for k in order + [0]:
            send_buf[m, k] = fold[k * block : (k + 1) * block, :].astype(jnp.bfloat16)

    def exchange(m, k, source, target, ssem, rsem, device):
        return pltpu.make_async_remote_copy(
            source.at[m, k], target.at[m, k], ssem.at[m, k], rsem.at[m, k], **to(device)
        )

    def sent(m, k):
        return exchange(m, k, send_buf, mine_buf, out_send, out_recv, peer(k))

    def passed(m, k):
        source = mine_buf if k else send_buf
        return exchange(m, k, source, theirs_buf, pass_send, pass_recv, partner)

    def returned(m, k):
        return exchange(m, k, ret_buf, ret_recv, ret_send, ret_rsem, peer(k))

    def swapped(m, j):
        return exchange(m, j, part_send, part_recv, part_ssem, part_rsem, partner)

    def first_half(m, allowed, chooser):
        for step in range(1, reach + 1):
            for which in range(2):
                kv_copies[m, step, which].wait_recv()
        if m == 0:
            for load in loads:
                load.wait()
        attend(m, allowed)
        normalize(m)
        pack(m, chooser)
        if m == 0:
            for k in order:
                sent(m, k).start()
        passed(m, 0).start()

    def lay_rows(at):
        for j in range(lanes):
            rows_buf[at : at + slots, j * 128 : (j + 1) * 128] = fold[
                pl.ds(j, slots, stride=lanes), :
            ].astype(jnp.bfloat16)

    def gather_rows(m):
        fold[0:block, :] = send_buf[m, 0].astype(jnp.float32)
        for k in order:
            sent(m, k).wait_recv()
            passed(m, k).start()
            if m + 1 < micros:
                sent(m + 1, k).start()
            fold[k * block : (k + 1) * block, :] = mine_buf[m, k].astype(jnp.float32)
        lay_rows(0)
        for k in [0] + order:
            passed(m, k).wait_recv()
            fold[k * block : (k + 1) * block, :] = theirs_buf[m, k].astype(jnp.float32)
        lay_rows(slots)

    tile = tile_of(units)

    def hidden_tile(start, size):
        rows = rows_buf[...]
        at = pl.ds(start, size)
        gate = lax.dot_general(
            rows, gate_buf[at, :], by_rows, preferred_element_type=jnp.float32
        )
        upward = lax.dot_general(
            rows, up_buf[at, :], by_rows, preferred_element_type=jnp.float32
        )
        hidden[:, at] = (gate / (1.0 + jnp.exp(-gate)) * upward).astype(jnp.bfloat16)

    def experts(m):
        for i in range(units // tile):
            hidden_tile(i * tile, tile)
        for j in range(width // chunk):
            at = slice(j * chunk, (j + 1) * chunk)
            added = jnp.dot(hidden[...], down_buf[:, at], preferred_element_type=jnp.float32)
            added = added.astype(jnp.bfloat16)
            part_own[j] = added[0:slots, :]
            part_send[m, j] = added[slots : 2 * slots, :]
            swapped(m, j).start()

    def give_back(m):
        for j in range(width // chunk):
            swapped(m, j).wait_recv()
            total = part_own[j].astype(jnp.float32) + part_recv[m, j].astype(jnp.float32)
            for i in range(per_chunk):
                fold[pl.ds(j * per_chunk + i, slots, stride=lanes), :] = total[
                    :, i * 128 : (i + 1) * 128
                ]
        for k in order + [0]:
            ret_buf[m, k] = fold[k * block : (k + 1) * block, :].astype(jnp.bfloat16)
        for k in order:
            returned(m, k).start()

    def combine(m, parts):
        fold[0:block, :] = ret_buf[m, 0].astype(jnp.float32)
        for k in order:
            returned(m, k).wait_recv()
            fold[k * block : (k + 1) * block, :] = ret_recv[m, k].astype(jnp.float32)
        for j in range(width // chunk):
            pieces = [
                fold[pl.ds(j * per_chunk + i, slots, stride=lanes), :].astype(jnp.bfloat16)
                for i in range(per_chunk)
            ]
            both = jnp.dot(
                parts, jnp.concatenate(pieces, axis=1), preferred_element_type=jnp.float32
            )
            at = slice(j * chunk, (j + 1) * chunk)
            out_ref[m, :, at] = (mixed[m, :, at] + (both[0:tok] + both[tok : 2 * tok])).astype(
                jnp.bfloat16
            )

    for m in range(micros):
        first_half(m, masks[m], maps[m][0])
    for m in range(micros):
        gather_rows(m)
        if m == 0:
            for load in weight_loads:
                load.wait()
        experts(m)
        give_back(m)
    for m in range(micros):
        combine(m, maps[m][1])
    for m in range(micros):
        for step in range(1, reach + 1):
            for which in range(2):
                kv_copies[m, step, which].wait_send()
        for k in order:
            sent(m, k).wait_send()
            returned(m, k).wait_send()
        for k in [0] + order:
            passed(m, k).wait_send()
        for j in range(width // chunk):
            swapped(m, j).wait_send()


def whole_layer(
    queries,
    key_rows,
    value_rows,
    residual,
    segment_ids,
    routes,
    route_weights,
    norm_gain,
    norm_bias,
    w_gate,
    w_up,
    w_down,
):
    count = lax.axis_size("wide")
    micros, tok, width = queries.shape
    reach = micros * tok * count // 32 // tok
    kv_width = key_rows.shape[2]
    units = w_gate.shape[1]
    chips = count // 2
    slots = EXPERTS * C
    lanes = width // 128
    block = C * lanes
    span = (reach + 1) * tok
    chunk = min(1024, width)
    chunks = width // chunk
    near = pl.BlockSpec(memory_space=pltpu.VMEM)
    far = pl.BlockSpec(memory_space=pl.ANY)
    half = jnp.bfloat16
    full = jnp.float32
    exchange = pltpu.VMEM((micros, chips, block, 128), half)
    weight = pltpu.VMEM((units, width), half)
    dma = pltpu.SemaphoreType.DMA
    scratch = [
        pltpu.VMEM((micros, tok, width), half),
        pltpu.VMEM((micros, span, kv_width), half),
        pltpu.VMEM((micros, span, kv_width), half),
        pltpu.VMEM((micros, tok, width), half),
        weight,
        weight,
        weight,
        pltpu.VMEM((micros, tok, width), full),
        pltpu.VMEM((tok, width), half),
        pltpu.VMEM((slots * lanes, 128), full),
        exchange,
        exchange,
        exchange,
        pltpu.VMEM((2 * slots, width), half),
        pltpu.VMEM((2 * slots, units), half),
        pltpu.VMEM((chunks, slots, chunk), half),
        pltpu.VMEM((micros, chunks, slots, chunk), half),
        pltpu.VMEM((micros, chunks, slots, chunk), half),
        exchange,
        exchange,
        dma((2 + 2 * micros,)),
        dma((3,)),
        dma((micros, reach, 2)),
        dma((micros, reach, 2)),
        dma((micros, chips)),
        dma((micros, chips)),
        dma((micros, chips)),
        dma((micros, chips)),
        dma((micros, chunks)),
        dma((micros, chunks)),
        dma((micros, chips)),
        dma((micros, chips)),
    ]
    return pl.pallas_call(
        functools.partial(layer_kernel, (count, micros, tok, width, reach)),
        out_shape=jax.ShapeDtypeStruct((micros, tok, width), half),
        in_specs=[near] * 5 + [far] * 7,
        out_specs=near,
        scratch_shapes=scratch,
        compiler_params=pltpu.CompilerParams(
            collective_id=0, has_side_effects=True, vmem_limit_bytes=VMEM_MOST
        ),
        name="layer",
    )(
        segment_ids.reshape(-1, 128),
        jnp.transpose(routes, (0, 2, 1)),
        jnp.transpose(route_weights, (0, 2, 1)),
        norm_gain.reshape(1, width),
        norm_bias.reshape(1, width),
        queries,
        key_rows,
        value_rows,
        residual,
        w_gate.T,
        w_up.T,
        w_down,
    )


def solution(mesh):
    placed = (
        P("groups", "wide", None),
        P("groups", "wide", None),
        P("groups", "wide", None),
        P("groups", "wide", None),
        P("groups"),
        P("groups", "wide", None),
        P("groups", "wide", None),
        P(),
        P(),
        P(None, "wide"),
        P(None, "wide"),
        P("wide", None),
    )
    wide_count = mesh.shape["wide"]
    paired = wide_count == 2 * EXPERTS

    def layer(*args):
        return whole_layer(*args) if paired else shards(*args)

    return jax.shard_map(
        layer, mesh=mesh, in_specs=placed, out_specs=P("groups", "wide", None), check_vma=False
    )
```

```python
import functools
import math

import jax
import jax.numpy as jnp
from jax import lax
from jax.experimental import pallas as pl
from jax.experimental.pallas import tpu as pltpu
from jax.sharding import PartitionSpec as P

HEADS = 32
KVH = 8
HD = 128
EXPERTS = 16
TOP = 2
C = 5


def passed_along(x, axis, by):
    length = lax.axis_size(axis)
    return lax.ppermute(x, axis, [(i, (i + by) % length) for i in range(length)])


def slot_targets(flat):
    onehot = (flat[..., None] == jnp.arange(EXPERTS, dtype=jnp.int32)).astype(jnp.int32)
    rank = jnp.cumsum(onehot, axis=-2) - 1
    slot = jnp.sum(onehot * rank, axis=-1)
    return flat * C + slot


UNITS_MOST = 400
VMEM_BYTES = 48 * 1024 * 1024
VMEM_MOST = 56 * 1024 * 1024


def tile_of(size):
    fits = [t for t in range(16, UNITS_MOST + 1, 16) if size % t == 0]
    return fits[-1] if fits else size


def expert_kernel(parts, *refs):
    row_refs = refs[:parts]
    gate_ref, up_ref, down_ref = refs[parts : parts + 3]
    out_refs = refs[parts + 3 : 2 * parts + 3]
    total = refs[2 * parts + 3]
    step = pl.program_id(0)
    last = pl.num_programs(0) - 1
    by_rows = (((1,), (1,)), ((), ()))
    rows = jnp.concatenate([ref[...] for ref in row_refs], axis=0)
    gate = lax.dot_general(rows, gate_ref[...], by_rows, preferred_element_type=jnp.float32)
    upward = lax.dot_general(rows, up_ref[...], by_rows, preferred_element_type=jnp.float32)
    hidden = (gate / (1.0 + jnp.exp(-gate)) * upward).astype(jnp.bfloat16)
    count = rows.shape[0] // parts
    added = jnp.dot(hidden, down_ref[...], preferred_element_type=jnp.float32)

    @pl.when(step == 0)
    def _():
        total[...] = added

    @pl.when(step > 0)
    def _():
        total[...] += added

    @pl.when(step == last)
    def _():
        for part in range(parts):
            block = total[part * count : (part + 1) * count, :]
            out_refs[part][...] = block.astype(jnp.bfloat16)


def compute_expert(row_parts, w_gate, w_up, w_down):
    parts = len(row_parts)
    count, width = row_parts[0].shape
    units = w_gate.shape[1]
    tile = tile_of(units)
    total = parts * count
    row_spec = pl.BlockSpec((count, width), lambda i: (0, 0))
    weight_spec = pl.BlockSpec((tile, width), lambda i: (i, 0))
    return pl.pallas_call(
        functools.partial(expert_kernel, parts),
        grid=(units // tile,),
        in_specs=[row_spec] * parts + [weight_spec] * 3,
        out_specs=[row_spec] * parts,
        out_shape=[jax.ShapeDtypeStruct((count, width), jnp.bfloat16)] * parts,
        scratch_shapes=[pltpu.VMEM((total, width), jnp.float32)],
        compiler_params=pltpu.CompilerParams(vmem_limit_bytes=VMEM_BYTES),
        cost_estimate=pl.CostEstimate(
            flops=6 * total * width * units,
            bytes_accessed=6 * width * units + 4 * total * width,
            transcendentals=total * units,
        ),
        name="expert",
    )(*row_parts, w_gate.T, w_up.T, w_down)


def shards(
    queries,
    key_rows,
    value_rows,
    residual,
    segment_ids,
    routes,
    route_weights,
    norm_gain,
    norm_bias,
    w_gate,
    w_up,
    w_down,
):
    wide_count = lax.axis_size("wide")
    device_index = lax.axis_index("wide")
    micro_count, tok_local, width = queries.shape
    tokens_micro = tok_local * wide_count
    doc_longest = micro_count * tokens_micro // 32
    scale = 1.0 / math.sqrt(HD)
    reach = doc_longest // tok_local
    group = HEADS // KVH
    steps_back = list(range(reach, 0, -1))
    received = []
    for step in steps_back:
        received.append(passed_along((key_rows, value_rows), "wide", step))
    span = (reach + 1) * tok_local
    before = jnp.full((reach * tok_local,), -1, jnp.int32)
    segments = jnp.concatenate([before, segment_ids])
    key_place = jnp.arange(span, dtype=jnp.int32) - reach * tok_local
    causal = key_place[None, :] <= jnp.arange(tok_local, dtype=jnp.int32)[:, None]
    results = []
    for local_micro in range(micro_count):
        earlier = max(local_micro - 1, 0)
        key_parts = []
        value_parts = []
        for position, step in enumerate(steps_back):
            key_far, value_far = received[position]
            crossed = device_index < step
            key_parts.append(jnp.where(crossed, key_far[earlier], key_far[local_micro]))
            value_parts.append(jnp.where(crossed, value_far[earlier], value_far[local_micro]))
        key_parts.append(key_rows[local_micro])
        value_parts.append(value_rows[local_micro])
        window_keys = jnp.concatenate(key_parts, axis=0)
        window_values = jnp.concatenate(value_parts, axis=0)
        key_seg = lax.dynamic_slice(
            segments, (local_micro * tokens_micro + device_index * tok_local,), (span,)
        )
        query_seg = key_seg[reach * tok_local :]
        allowed = (key_seg[None, :] == query_seg[:, None]) & causal
        query_now = queries[local_micro].reshape(tok_local, KVH, group, HD)
        scores = (
            jnp.einsum(
                "tkgd,skd->kgts",
                query_now,
                window_keys.reshape(span, KVH, HD),
                preferred_element_type=jnp.float32,
            )
            * scale
        )
        scores = jnp.where(allowed[None, None], scores, -1e30)
        top = jnp.max(scores, axis=3, keepdims=True)
        expo = jnp.exp(scores - top)
        probs = (expo / jnp.sum(expo, axis=3, keepdims=True)).astype(jnp.bfloat16)
        result = jnp.einsum(
            "kgts,skd->tkgd",
            probs,
            window_values.reshape(span, KVH, HD),
            preferred_element_type=jnp.float32,
        ).astype(jnp.bfloat16)
        results.append(result.reshape(tok_local, width))
    team = wide_count // EXPERTS
    across = [[e * team + r for e in range(EXPERTS)] for r in range(team)]
    inside = [[e * team + r for r in range(team)] for e in range(EXPERTS)]
    swap = [(i, i ^ 1) for i in range(wide_count)]
    fold = (width // 128, 128)
    slots = EXPERTS * C

    def exchanged(x):
        sent = x.reshape(EXPERTS, C, *fold)
        return lax.all_to_all(sent, "wide", 0, 0, axis_index_groups=across, tiled=True)

    state = []
    for micro in range(micro_count):
        mixed = residual[micro].astype(jnp.float32) + results[micro].astype(jnp.float32)
        center = mixed - jnp.mean(mixed, axis=-1, keepdims=True)
        variance = jnp.mean(center * center, axis=-1, keepdims=True)
        normed = (center / jnp.sqrt(variance + 1e-05) * norm_gain + norm_bias).astype(
            jnp.bfloat16
        )
        target = slot_targets(routes[micro].reshape(tok_local * TOP)).reshape(tok_local, TOP)
        hits = target[..., None] == jnp.arange(slots, dtype=jnp.int32)
        chooser = jnp.any(hits, axis=1).astype(jnp.bfloat16)
        packed = jnp.einsum(
            "te,td->ed", chooser, normed, preferred_element_type=jnp.float32
        ).astype(jnp.bfloat16)
        state.append((mixed, hits, exchanged(packed).reshape(slots, *fold)))
    outputs = []
    for micro in range(micro_count):
        mixed, hits, landed = state[micro]
        if team == 2:
            other = lax.ppermute(landed, "wide", swap)
            pair = (landed.reshape(slots, width), other.reshape(slots, width))
            mine, theirs = compute_expert(pair, w_gate, w_up, w_down)
            theirs = lax.ppermute(theirs, "wide", swap)
            summed = mine.astype(jnp.float32) + theirs.astype(jnp.float32)
        else:
            rows = lax.all_gather(landed, "wide", axis_index_groups=inside, tiled=True)
            rows = rows.reshape(team * slots, width)
            (partial_value,) = compute_expert((rows,), w_gate, w_up, w_down)
            blocks = lax.all_to_all(
                partial_value.reshape(team, slots, *fold),
                "wide",
                0,
                0,
                axis_index_groups=inside,
                tiled=True,
            )
            summed = blocks.astype(jnp.float32).sum(axis=0).reshape(slots, width)
        returned = exchanged(summed.astype(jnp.bfloat16)).reshape(slots, width)
        shares = jnp.sum(jnp.where(hits, route_weights[micro][..., None], 0.0), axis=1)
        high = shares.astype(jnp.bfloat16)
        low = (shares - high.astype(jnp.float32)).astype(jnp.bfloat16)
        mixture = jnp.dot(high, returned, preferred_element_type=jnp.float32) + jnp.dot(
            low, returned, preferred_element_type=jnp.float32
        )
        outputs.append((mixed + mixture).astype(jnp.bfloat16))
    return jnp.stack(outputs)


MESH_ID = pl.DeviceIdType.MESH


def flipped(place, by, bits):
    total = 0
    for bit in range(bits):
        own = (place // (1 << bit)) % 2
        total = total + ((own + (by >> bit) % 2) % 2) * (1 << bit)
    return total


def column_of(row):
    size = row.shape[1]
    down = lax.broadcasted_iota(jnp.int32, (size, size), 0)
    across = lax.broadcasted_iota(jnp.int32, (size, size), 1)
    spread = jnp.broadcast_to(row, (size, size))
    return jnp.sum(jnp.where(down == across, spread, 0.0), axis=1, keepdims=True)


def layer_kernel(
    sizes,
    seg_ref,
    routes_ref,
    shares_ref,
    gain_ref,
    bias_ref,
    q_hbm,
    k_hbm,
    v_hbm,
    res_hbm,
    gate_hbm,
    up_hbm,
    down_hbm,
    out_ref,
    q_buf,
    k_win,
    v_win,
    res_buf,
    gate_buf,
    up_buf,
    down_buf,
    mixed,
    normed,
    fold,
    send_buf,
    mine_buf,
    rows_buf,
    hidden,
    part_own,
    part_send,
    part_recv,
    ret_buf,
    ret_recv,
    load_sem,
    weight_sem,
    kv_send,
    kv_recv,
    out_send,
    out_recv,
    pass_send,
    pass_recv,
    part_ssem,
    part_rsem,
    ret_send,
    ret_rsem,
):
    count, micros, tok, width, reach = sizes
    chips = count // 2
    bits = chips.bit_length() - 1
    lanes = width // 128
    slots = EXPERTS * C
    block = C * lanes
    group = HEADS // KVH
    span = (reach + 1) * tok
    units = gate_hbm.shape[0]
    me = lax.axis_index("wide")
    chip = me // 2
    core = me % 2
    partner = chip * 2 + (1 - core)
    order = list(range(chips - 1, 0, -1))

    def peer(k):
        return flipped(chip, k, bits) * 2 + core

    def to(device):
        return dict(device_id={"wide": device}, device_id_type=MESH_ID)

    loads = [
        pltpu.make_async_copy(q_hbm, q_buf, load_sem.at[0]),
        pltpu.make_async_copy(res_hbm, res_buf, load_sem.at[1]),
    ]
    for m in range(micros):
        own = pl.ds(reach * tok, tok)
        loads.append(pltpu.make_async_copy(k_hbm.at[m], k_win.at[m, own], load_sem.at[2 + 2 * m]))
        loads.append(pltpu.make_async_copy(v_hbm.at[m], v_win.at[m, own], load_sem.at[3 + 2 * m]))
    for load in loads:
        load.start()

    barrier = pltpu.get_barrier_semaphore()

    def greet(step, carry):
        pl.semaphore_signal(barrier, inc=1, **to((me + step) % count))
        return carry

    lax.fori_loop(1, count, greet, 0)

    def allowed_of(m):
        start = m * tok * count + me * tok - reach * tok
        rows = seg_ref.shape[0]
        first = (start + rows * 128) // 128
        both = jnp.concatenate(
            [seg_ref[pl.ds(first % rows, 1), :], seg_ref[pl.ds((first + 1) % rows, 1), :]],
            axis=1,
        )
        shift = (start + rows * 128) % 128
        seg = both[:, 0:span]
        for skip in range(tok, 128, tok):
            picked = (jnp.zeros((1, span), jnp.int32) + shift) == skip
            seg = jnp.where(picked, both[:, skip : skip + span], seg)
        seg = seg.astype(jnp.float32)
        query_seg = column_of(seg[:, reach * tok :])
        place = lax.broadcasted_iota(jnp.int32, (tok, span), 1)
        now = lax.broadcasted_iota(jnp.int32, (tok, span), 0)
        fits = jnp.broadcast_to(seg, (tok, span)) == jnp.broadcast_to(query_seg, (tok, span))
        fits = fits & (place <= now + reach * tok) & (place + start >= 0)
        return jnp.concatenate([jnp.where(fits, 1.0, 0.0)] * group, axis=0)

    def slot_maps(m):
        names = routes_ref[m].astype(jnp.float32)
        row_names = [names[i : i + 1, :] for i in range(TOP)]
        col_names = [column_of(row) for row in row_names]
        weights = [column_of(shares_ref[m][i : i + 1, :]) for i in range(TOP)]
        before = lax.broadcasted_iota(jnp.int32, (tok, tok), 0)
        after = lax.broadcasted_iota(jnp.int32, (tok, tok), 1)

        def slot_rows(i):
            total = jnp.zeros((tok, tok), jnp.float32)
            for other in range(TOP):
                same = (col_names[other] == row_names[i]) & (before < after)
                total = total + jnp.where(same, 1.0, 0.0)
            return jnp.sum(total, axis=0, keepdims=True)

        def slot_cols(i):
            total = jnp.zeros((tok, tok), jnp.float32)
            for other in range(TOP):
                same = (row_names[other] == col_names[i]) & (after < before)
                total = total + jnp.where(same, 1.0, 0.0)
            return jnp.sum(total, axis=1, keepdims=True)

        def places(shape, axis, low=0):
            at = lax.broadcasted_iota(jnp.int32, shape, axis) + low
            turn = jnp.zeros(shape, jnp.int32)
            for k in range(1, EXPERTS):
                turn = turn + jnp.where(at >= k * C, 1, 0)
            expert = jnp.bitwise_xor(turn, jnp.zeros(shape, jnp.int32) + chip)
            return expert.astype(jnp.float32), (at - turn * C).astype(jnp.float32)

        expert, slot = places((slots, tok), 0)
        chooser = jnp.zeros((slots, tok), jnp.float32)
        for i in range(TOP):
            chooser = chooser + jnp.where(
                (expert == row_names[i]) & (slot == slot_rows(i)), 1.0, 0.0
            )
        halves = []
        for low in (0, slots // 2):
            expert, slot = places((tok, slots // 2), 1, low)
            parts = jnp.zeros((tok, slots // 2), jnp.float32)
            for i in range(TOP):
                parts = parts + jnp.where(
                    (expert == col_names[i]) & (slot == slot_cols(i)), weights[i], 0.0
                )
            high = parts.astype(jnp.bfloat16)
            rest = (parts - high.astype(jnp.float32)).astype(jnp.bfloat16)
            halves.append(jnp.concatenate([high, rest], axis=0))
        return chooser.astype(jnp.bfloat16), halves

    masks = [allowed_of(m) for m in range(micros)]
    maps = [slot_maps(m) for m in range(micros)]
    pl.semaphore_wait(barrier, count - 1)

    def neighbour(m, step, which):
        far, win = ((k_hbm, k_win), (v_hbm, v_win))[which]
        crossed = (me + step) // count
        return pltpu.make_async_remote_copy(
            far.at[(m + micros - crossed) % micros],
            win.at[m, pl.ds((reach - step) * tok, tok)],
            kv_send.at[m, step - 1, which],
            kv_recv.at[m, step - 1, which],
            **to((me + step) % count),
        )

    def send_window(m):
        for which in range(2):
            for step in range(1, reach + 1):
                neighbour(m, step, which).start()

    def await_window(m, which):
        for step in range(1, reach + 1):
            neighbour(m, step, which).wait_recv()

    send_window(0)
    weight_loads = [
        pltpu.make_async_copy(far, near, weight_sem.at[i])
        for i, (far, near) in enumerate(
            ((gate_hbm, gate_buf), (up_hbm, up_buf), (down_hbm, down_buf))
        )
    ]
    for load in weight_loads:
        load.start()

    by_rows = (((1,), (1,)), ((), ()))
    scale = 1.0 / math.sqrt(HD)

    def attend(m, allowed):
        together = KVH // 2
        for start in range(0, KVH, together):
            heads = range(start, start + together)
            cols = [slice(head * HD, (head + 1) * HD) for head in heads]
            scores = []
            for head, at in zip(heads, cols):
                queries = [
                    q_buf[m, :, (head * group + g) * HD : (head * group + g + 1) * HD]
                    for g in range(group)
                ]
                scores.append(
                    lax.dot_general(
                        jnp.concatenate(queries, axis=0),
                        k_win[m, :, at],
                        by_rows,
                        preferred_element_type=jnp.float32,
                    )
                )
            scores = [jnp.where(allowed > 0.5, score * scale, -1e30) for score in scores]
            tops = [jnp.max(score, axis=1, keepdims=True) for score in scores]
            expos = [jnp.exp(score - top) for score, top in zip(scores, tops)]
            sums = [jnp.sum(expo, axis=1, keepdims=True) for expo in expos]
            if start == 0:
                await_window(m, 1)
            probs = [(expo / total).astype(jnp.bfloat16) for expo, total in zip(expos, sums)]
            results = [
                jnp.dot(prob, v_win[m, :, at], preferred_element_type=jnp.float32)
                for prob, at in zip(probs, cols)
            ]
            for head, result in zip(heads, results):
                result = result.astype(jnp.bfloat16).astype(jnp.float32)
                for g in range(group):
                    at = slice((head * group + g) * HD, (head * group + g + 1) * HD)
                    mixed[m, :, at] = (
                        res_buf[m, :, at].astype(jnp.float32) + result[g * tok : (g + 1) * tok, :]
                    )

    def normalize(m):
        values = mixed[m]
        center = values - jnp.mean(values, axis=1, keepdims=True)
        variance = jnp.mean(center * center, axis=1, keepdims=True)
        scaled = center * (1.0 / jnp.sqrt(variance + 1e-05))
        normed[...] = (scaled * gain_ref[...] + bias_ref[...]).astype(jnp.bfloat16)

    chunk = min(1024, width)
    per_chunk = chunk // 128

    def pack(m, chooser):
        for j in range(width // chunk):
            packed = jnp.dot(
                chooser, normed[:, j * chunk : (j + 1) * chunk], preferred_element_type=jnp.float32
            )
            for i in range(per_chunk):
                fold[pl.ds(j * per_chunk + i, slots, stride=lanes), :] = packed[
                    :, i * 128 : (i + 1) * 128
                ]
        for k in order + [0]:
            send_buf[m, k] = fold[k * block : (k + 1) * block, :].astype(jnp.bfloat16)

    def exchange(m, k, source, target, ssem, rsem, device):
        return pltpu.make_async_remote_copy(
            source.at[m, k], target.at[m, k], ssem.at[m, k], rsem.at[m, k], **to(device)
        )

    def sent(m, k):
        return exchange(m, k, send_buf, mine_buf, out_send, out_recv, peer(k))

    def passed(m, j):
        cols = pl.ds(j * chunk, chunk)
        return pltpu.make_async_remote_copy(
            rows_buf.at[m, pl.ds(0, slots), cols],
            rows_buf.at[m, pl.ds(slots, slots), cols],
            pass_send.at[m, j],
            pass_recv.at[m, j],
            **to(partner),
        )

    def returned(m, k):
        return exchange(m, k, ret_buf, ret_recv, ret_send, ret_rsem, peer(k))

    def swapped(m, j):
        return exchange(m, j, part_send, part_recv, part_ssem, part_rsem, partner)

    def first_half(m, allowed, chooser):
        await_window(m, 0)
        if m + 1 < micros:
            send_window(m + 1)
        if m == 0:
            for load in loads:
                load.wait()
        attend(m, allowed)
        normalize(m)
        pack(m, chooser)
        if m == 0:
            for k in order:
                sent(m, k).start()

    lag = chips // 2 - 2

    def gather_rows(m):
        fold[0:block, :] = send_buf[m, 0].astype(jnp.float32)
        waiting = list(order)
        for turn, k in enumerate(order):
            sent(m, k).wait_recv()
            if m + 1 < micros and turn >= lag:
                sent(m + 1, waiting.pop(0)).start()
            fold[k * block : (k + 1) * block, :] = mine_buf[m, k].astype(jnp.float32)
        if m + 1 < micros:
            for k in waiting:
                sent(m + 1, k).start()
        for j in range(width // chunk):
            for i in range(j * per_chunk, (j + 1) * per_chunk):
                rows_buf[m, 0:slots, i * 128 : (i + 1) * 128] = fold[
                    pl.ds(i, slots, stride=lanes), :
                ].astype(jnp.bfloat16)
            passed(m, j).start()

    tile = tile_of(units)

    def hidden_tile(m, start, size):
        rows = rows_buf[m]
        at = pl.ds(start, size)
        gate = lax.dot_general(
            rows, gate_buf[at, :], by_rows, preferred_element_type=jnp.float32
        )
        upward = lax.dot_general(
            rows, up_buf[at, :], by_rows, preferred_element_type=jnp.float32
        )
        hidden[:, at] = (gate / (1.0 + jnp.exp(-gate)) * upward).astype(jnp.bfloat16)

    def upward_half(m):
        for j in range(width // chunk):
            passed(m, j).wait_recv()
        for i in range(units // tile):
            hidden_tile(m, i * tile, tile)

    def downward_half(m):
        for j in range(width // chunk):
            at = slice(j * chunk, (j + 1) * chunk)
            added = jnp.dot(hidden[...], down_buf[:, at], preferred_element_type=jnp.float32)
            added = added.astype(jnp.bfloat16)
            part_own[j] = added[0:slots, :]
            part_send[m, j] = added[slots : 2 * slots, :]
            swapped(m, j).start()

    def give_back(m):
        for j in range(width // chunk):
            swapped(m, j).wait_recv()
            total = part_own[j].astype(jnp.float32) + part_recv[m, j].astype(jnp.float32)
            for i in range(per_chunk):
                fold[pl.ds(j * per_chunk + i, slots, stride=lanes), :] = total[
                    :, i * 128 : (i + 1) * 128
                ]
        for k in order + [0]:
            ret_buf[m, k] = fold[k * block : (k + 1) * block, :].astype(jnp.bfloat16)
        for k in order:
            returned(m, k).start()

    def mixture(parts, low, rows, j):
        pieces = [
            fold[pl.ds(low * lanes + j * per_chunk + i, rows, stride=lanes), :]
            for i in range(per_chunk)
        ]
        pieces = [piece.astype(jnp.bfloat16) for piece in pieces]
        both = jnp.dot(parts, jnp.concatenate(pieces, axis=1), preferred_element_type=jnp.float32)
        return both[0:tok] + both[tok : 2 * tok]

    def combine(m, parts):
        middle = slots // 2
        for turn, k in enumerate(order + [0]):
            if k:
                returned(m, k).wait_recv()
                landed = ret_recv[m, k]
            else:
                landed = ret_buf[m, 0]
            fold[k * block : (k + 1) * block, :] = landed.astype(jnp.float32)
            if turn + 1 == chips // 2:
                for j in range(width // chunk):
                    at = slice(j * chunk, (j + 1) * chunk)
                    mixed[m, :, at] = mixed[m, :, at] + mixture(parts[1], middle, middle, j)
        for j in range(width // chunk):
            at = slice(j * chunk, (j + 1) * chunk)
            out_ref[m, :, at] = (mixed[m, :, at] + mixture(parts[0], 0, middle, j)).astype(
                jnp.bfloat16
            )

    for m in range(micros):
        first_half(m, masks[m], maps[m][0])
    gather_rows(0)
    for load in weight_loads:
        load.wait()
    for m in range(micros):
        upward_half(m)
        downward_half(m)
        give_back(m)
        if m + 1 < micros:
            gather_rows(m + 1)
    for m in range(micros):
        if m + 1 == micros:
            for i in range(micros):
                for step in range(1, reach + 1):
                    for which in range(2):
                        neighbour(i, step, which).wait_send()
                for k in order:
                    sent(i, k).wait_send()
                    if i < m:
                        returned(i, k).wait_send()
                for j in range(width // chunk):
                    passed(i, j).wait_send()
                    swapped(i, j).wait_send()
        combine(m, maps[m][1])
    for k in order:
        returned(micros - 1, k).wait_send()


def whole_layer(
    queries,
    key_rows,
    value_rows,
    residual,
    segment_ids,
    routes,
    route_weights,
    norm_gain,
    norm_bias,
    w_gate,
    w_up,
    w_down,
):
    count = lax.axis_size("wide")
    micros, tok, width = queries.shape
    reach = micros * tok * count // 32 // tok
    kv_width = key_rows.shape[2]
    units = w_gate.shape[1]
    chips = count // 2
    slots = EXPERTS * C
    lanes = width // 128
    block = C * lanes
    span = (reach + 1) * tok
    chunk = min(1024, width)
    chunks = width // chunk
    near = pl.BlockSpec(memory_space=pltpu.VMEM)
    far = pl.BlockSpec(memory_space=pl.ANY)
    half = jnp.bfloat16
    full = jnp.float32
    exchange = pltpu.VMEM((micros, chips, block, 128), half)
    weight = pltpu.VMEM((units, width), half)
    dma = pltpu.SemaphoreType.DMA
    scratch = [
        pltpu.VMEM((micros, tok, width), half),
        pltpu.VMEM((micros, span, kv_width), half),
        pltpu.VMEM((micros, span, kv_width), half),
        pltpu.VMEM((micros, tok, width), half),
        weight,
        weight,
        weight,
        pltpu.VMEM((micros, tok, width), full),
        pltpu.VMEM((tok, width), half),
        pltpu.VMEM((slots * lanes, 128), full),
        exchange,
        exchange,
        pltpu.VMEM((micros, 2 * slots, width), half),
        pltpu.VMEM((2 * slots, units), half),
        pltpu.VMEM((chunks, slots, chunk), half),
        pltpu.VMEM((micros, chunks, slots, chunk), half),
        pltpu.VMEM((micros, chunks, slots, chunk), half),
        exchange,
        exchange,
        dma((2 + 2 * micros,)),
        dma((3,)),
        dma((micros, reach, 2)),
        dma((micros, reach, 2)),
        dma((micros, chips)),
        dma((micros, chips)),
        dma((micros, chunks)),
        dma((micros, chunks)),
        dma((micros, chunks)),
        dma((micros, chunks)),
        dma((micros, chips)),
        dma((micros, chips)),
    ]
    return pl.pallas_call(
        functools.partial(layer_kernel, (count, micros, tok, width, reach)),
        out_shape=pltpu.VMEM((micros, tok, width), half),
        in_specs=[near] * 5 + [far] * 7,
        out_specs=near,
        scratch_shapes=scratch,
        compiler_params=pltpu.CompilerParams(
            collective_id=0, has_side_effects=True, vmem_limit_bytes=VMEM_MOST
        ),
        name="layer",
    )(
        segment_ids.reshape(-1, 128),
        jnp.transpose(routes, (0, 2, 1)),
        jnp.transpose(route_weights, (0, 2, 1)),
        norm_gain.reshape(1, width),
        norm_bias.reshape(1, width),
        queries,
        key_rows,
        value_rows,
        residual,
        w_gate.T,
        w_up.T,
        w_down,
    )


def solution(mesh):
    placed = (
        P("groups", "wide", None),
        P("groups", "wide", None),
        P("groups", "wide", None),
        P("groups", "wide", None),
        P("groups"),
        P("groups", "wide", None),
        P("groups", "wide", None),
        P(),
        P(),
        P(None, "wide"),
        P(None, "wide"),
        P("wide", None),
    )
    wide_count = mesh.shape["wide"]
    paired = wide_count == 2 * EXPERTS

    def layer(*args):
        return whole_layer(*args) if paired else shards(*args)

    return jax.shard_map(
        layer, mesh=mesh, in_specs=placed, out_specs=P("groups", "wide", None), check_vma=False
    )
```
